32 devices in a mesh: frame: 8 (over z, x), feat: 4 (over y, core).
Axes of the slice: x: 2, y: 2, z: 4, core: 2. Of those that a mesh axis runs over, the one named last changes fastest.
Arguments:
- coords: bfloat16 [8, 64, 3, 128], P('frame', 'feat'), may hold values from -9 to 9
- walker_map: int32 [8, 64], P('frame', 'feat'), may hold values from 0 to 63, each once within a row
- pairs: int32 [2, 16384], P(None, 'feat'), may hold values from 0 to 127, as said below
Outputs:
- inst_cov: float32 [16384, 16384], P('feat', 'frame')
- lag_cov: float32 [16384, 16384], P('feat', 'frame')
The draws below stay inside these ranges and needn't reach their ends.
Inputs may be any that keep to these rules, and one draw needn't show every extreme that they name: `pairs`: the two blocks of a feature differ.
All inputs are finite; a program needn't handle non-finite values.
Results may differ from the reference program's by a relative error of at most 0.0038.
Values may be sent and summed in bfloat16 or wider, within the bound.
No kernel may reach another device: no remote copies, remote signals or barrier semaphores. Data moves between devices by JAX's collectives and lax.ppermute only.
A program may use at most 128 MiB of HBM per device.

```python
import jax
import jax.numpy as jnp
from jax import lax

REPLICAS = 64
BLOCKS = 128
FEATURES = 16384
FRAMES = 8
LAG = 2


def draw_pairs(key, part):
    key_first, key_step = jax.random.split(jax.random.fold_in(key, 11))
    first = jax.random.randint(key_first, (FEATURES,), 0, BLOCKS)
    offset = jax.random.randint(key_step, (FEATURES,), 1, BLOCKS)
    second = (first + offset) % BLOCKS
    return jnp.stack([first, second]).astype(jnp.int32)


def block_levels(rng, extent, cuts, least, largest):
    def one(position, parts):
        heights = jax.random.uniform(jax.random.fold_in(jax.random.fold_in(rng, 6), position), (parts,), jnp.float32, least / len(cuts), largest / len(cuts))
        return jnp.repeat(jnp.exp(heights), extent[position] // parts).reshape((-1,) + (1,) * (len(extent) - position - 1))

    loudness = one(*cuts[0])
    for cut in cuts[1:]:
        loudness = loudness * one(*cut)
    return loudness


def noise(own_key, dims, scale, most, pieces=(), kind=jnp.bfloat16):
    entries = scale * jax.random.normal(own_key, dims, jnp.float32)
    if pieces:
        entries = entries * block_levels(own_key, dims, pieces, -0.22, 0.18)
    return jnp.clip(entries, -most, most).astype(kind)


def setup_inputs(seed: int = 0) -> dict:
    seeds = jax.random.split(jax.random.key(seed), 4)
    coords = noise(seeds[0], (FRAMES, REPLICAS, 3, BLOCKS), 1.5, 9.0, ((0, 8), (1, 4)))
    walker_map = jax.vmap(lambda own: jax.random.permutation(own, REPLICAS))(jax.random.split(seeds[1], FRAMES)).reshape((FRAMES, REPLICAS)).astype(jnp.int32)
    pairs = draw_pairs(jax.random.fold_in(seeds[3], 71), 0)
    return {"coords": coords, "walker_map": walker_map, "pairs": pairs}


def demux(coords, walker_map):
    count = walker_map.shape[1]
    labels = jnp.arange(count, dtype=jnp.int32)
    match = walker_map[:, :, None] == labels[None, None, :]
    inverse = lax.optimization_barrier(jnp.sum(jnp.where(match, labels[None, :, None], 0), axis=1)).astype(jnp.int32)
    return jnp.take_along_axis(coords, inverse[:, :, None, None], axis=1)

def reference(coords, walker_map, pairs):
    walker_coords = demux(coords, walker_map)

    def measure(frame_coords):
        values = frame_coords.astype(jnp.float32)
        diff = jnp.take(values, pairs[0], axis=-1) - jnp.take(values, pairs[1], axis=-1)
        return jnp.sqrt(lax.optimization_barrier(jnp.sum(diff * diff, axis=-2)))
    features = lax.map(measure, walker_coords)
    means = lax.optimization_barrier(jnp.mean(features, axis=(0, 1)))
    centered = (features - means).astype(jnp.bfloat16)
    flat = centered.reshape(-1, FEATURES)
    contract = (((0,), (0,)), ((), ()))
    inst_cov = lax.dot_general(flat, flat, contract, preferred_element_type=jnp.float32) / (FRAMES * REPLICAS)
    early = centered[:FRAMES - LAG].reshape(-1, FEATURES)
    late = centered[LAG:].reshape(-1, FEATURES)
    lag_cov = lax.dot_general(early, late, contract, preferred_element_type=jnp.float32) / ((FRAMES - LAG) * REPLICAS)
    return (inst_cov, lag_cov)
```

```python
import functools

import jax
import jax.numpy as jnp
from jax import lax
from jax.experimental import pallas as pl
from jax.experimental.pallas import tpu as pltpu
from jax.sharding import PartitionSpec as P

LANES = 128


def divisor(n, most):
    return max(d for d in range(1, min(n, most) + 1) if n % d == 0)


def swap(x, axis, bit):
    n = lax.axis_size(axis)
    return lax.ppermute(x, axis, [(i, i ^ bit) for i in range(n)])


def bits_down(n):
    return [1 << b for b in reversed(range(n.bit_length() - 1))]


def gather_all(block, pairs):
    frames, feats = lax.axis_size("frame"), lax.axis_size("feat")
    f, g = lax.axis_index("frame"), lax.axis_index("feat")
    lanes = block.shape[-1]
    held = block[None]
    for bit in bits_down(frames):
        got = swap(held, "frame", bit)
        held = jnp.stack([held, got], axis=1).reshape((-1,) + block.shape)
    share = frames // feats
    width = pairs.shape[1] // share
    piece = lax.dynamic_slice_in_dim(pairs, (f % share) * width, width, 1)
    piece = piece.astype(block.dtype).reshape(-1, lanes)
    wanted = f // share
    for bit in bits_down(feats):
        rows = held.reshape(-1, lanes)
        got = swap(jnp.concatenate([rows, piece], axis=0), "feat", bit)
        held = jnp.concatenate([held, got[: rows.shape[0]].reshape(held.shape)], axis=2)
        piece = jnp.where((wanted & bit) == (g & bit), piece, got[rows.shape[0] :])
    return held, piece


def onehot_rows(pairs_ref, out_ref):
    count, blocks = out_ref.shape
    ids = lax.broadcasted_iota(jnp.int32, (blocks, LANES), 0)
    for j in range(count // LANES):
        at = pl.ds(j * LANES, LANES)
        first = (ids == pairs_ref[0:1, at]).astype(jnp.float32)
        second = (ids == pairs_ref[1:2, at]).astype(jnp.float32)
        out_ref[at, :] = (first - second).T.astype(out_ref.dtype)


def covariances(
    lag, tile, chunk, f_ref, y_ref, rows_ref, cols_ref, inst_hbm, lag_hbm,
    x_ref, xt_ref, r_ref, l_ref, feat_ref, out_ref, sems,
):
    frames, _, replicas, blocks = y_ref.shape
    samples = frames * replicas
    row_width, col_width = rows_ref.shape[0], r_ref.shape[1]
    steps, chunks = row_width // tile, col_width // chunk
    early = (frames - lag) * replicas
    late = lag * replicas
    f = f_ref[0]

    walkers = lax.broadcasted_iota(jnp.int32, (replicas, replicas), 1)
    for t in range(frames):
        slab = y_ref.at[t ^ f]
        labels = slab[3][:, :replicas].astype(jnp.int32)
        match = (labels == walkers).astype(jnp.float32).astype(jnp.bfloat16)
        for c in range(3):
            x_ref[c, t * replicas : (t + 1) * replicas, :] = lax.dot_general(
                match, slab[c], (((0,), (0,)), ((), ())), preferred_element_type=jnp.float32
            ).astype(jnp.bfloat16)
    for c in range(3):
        xt_ref[c] = x_ref[c].astype(jnp.float32).T.astype(jnp.bfloat16)

    def distances(parts):
        total = parts[0] * parts[0] + parts[1] * parts[1] + parts[2] * parts[2]
        return jnp.sqrt(total)

    ids = lax.broadcasted_iota(jnp.int32, (blocks, LANES), 0).astype(jnp.float32)
    half = col_width // LANES
    for j in range(half):
        first = cols_ref[j : j + 1, :].astype(jnp.float32)
        second = cols_ref[half + j : half + j + 1, :].astype(jnp.float32)
        pick = (ids == first).astype(jnp.float32) - (ids == second).astype(jnp.float32)
        pick = pick.astype(jnp.bfloat16)
        values = distances(
            [jnp.dot(x_ref[c], pick, preferred_element_type=jnp.float32) for c in range(3)]
        )
        mean = jnp.sum(values, axis=0, keepdims=True) * (1.0 / samples)
        r_ref[:, j * LANES : (j + 1) * LANES] = (values - mean).astype(jnp.bfloat16)

    def left(step, slot):
        pick = rows_ref[pl.ds(pl.multiple_of(step * tile, tile), tile), :]
        values = distances(
            [jnp.dot(pick, xt_ref[c], preferred_element_type=jnp.float32) for c in range(3)]
        )
        mean = jnp.sum(values, axis=1, keepdims=True) * (1.0 / samples)
        l_ref[slot] = (values - mean).astype(jnp.bfloat16)

    def copies(step, slot, n):
        rows = pl.ds(pl.multiple_of(step * tile, tile), tile)
        at = pl.ds(n * chunk, chunk)
        return [
            pltpu.make_async_copy(
                out_ref.at[slot, o, :, at], hbm.at[rows, at], sems.at[slot, o, n]
            )
            for o, hbm in enumerate((inst_hbm, lag_hbm))
        ]

    def body(step, carry):
        slot = lax.rem(step, 2)
        left(step, 0)
        for n in range(chunks):
            at = slice(n * chunk, (n + 1) * chunk)

            @pl.when(step >= 2)
            def _():
                for copy in copies(step - 2, slot, n):
                    copy.wait()

            out_ref[slot, 0, :, at] = jnp.dot(
                l_ref[0], r_ref[:, at], preferred_element_type=jnp.float32
            ) * (1.0 / samples)
            out_ref[slot, 1, :, at] = jnp.dot(
                l_ref[0, :, :early], r_ref[late:, at], preferred_element_type=jnp.float32
            ) * (1.0 / early)
            for copy in copies(step, slot, n):
                copy.start()
        return carry

    lax.fori_loop(0, steps, body, 0)
    for step in range(max(steps - 2, 0), steps):
        for n in range(chunks):
            for copy in copies(step, step % 2, n):
                copy.wait()


def per_device(coords, walker_map, pairs):
    frames, feats = lax.axis_size("frame"), lax.axis_size("feat")
    blocks = coords.shape[3]
    row_width = pairs.shape[1]
    col_width = row_width * feats // frames
    labels = jnp.broadcast_to(walker_map[0][:, None], (walker_map.shape[1], blocks))
    block = jnp.concatenate(
        [jnp.swapaxes(coords[0], 0, 1), labels.astype(coords.dtype)[None]], axis=0
    )
    rows = pl.pallas_call(
        onehot_rows,
        out_shape=jax.ShapeDtypeStruct((row_width, blocks), jnp.bfloat16),
        cost_estimate=pl.CostEstimate(
            flops=4 * row_width * blocks, bytes_accessed=2 * row_width * blocks, transcendentals=0
        ),
    )(pairs)
    held, cols = gather_all(block, pairs)
    replicas = held.shape[2]
    samples = frames * replicas
    tile, chunk = divisor(row_width, 256), divisor(col_width, 512)
    vmem = pl.BlockSpec(memory_space=pltpu.VMEM)
    hbm = pl.BlockSpec(memory_space=pl.ANY)
    return pl.pallas_call(
        functools.partial(covariances, frames // 3, tile, chunk),
        out_shape=[jax.ShapeDtypeStruct((row_width, col_width), jnp.float32)] * 2,
        in_specs=[pl.BlockSpec(memory_space=pltpu.SMEM), vmem, vmem, vmem],
        out_specs=[hbm, hbm],
        scratch_shapes=[
            pltpu.VMEM((3, samples, blocks), jnp.bfloat16),
            pltpu.VMEM((3, blocks, samples), jnp.bfloat16),
            pltpu.VMEM((samples, col_width), jnp.bfloat16),
            pltpu.VMEM((2, tile, samples), jnp.bfloat16),
            pltpu.VMEM((8, LANES), jnp.float32),
            pltpu.VMEM((2, 2, tile, col_width), jnp.float32),
            pltpu.SemaphoreType.DMA((2, 2, col_width // chunk)),
        ],
        compiler_params=pltpu.CompilerParams(vmem_limit_bytes=48 << 20),
    )(lax.axis_index("frame").astype(jnp.int32).reshape(1), held, rows, cols)


def solution(mesh):
    in_specs = (P("frame", "feat", None, None), P("frame", "feat"), P(None, "feat"))
    out_specs = (P("feat", "frame"), P("feat", "frame"))
    return jax.shard_map(
        lambda *args: tuple(per_device(*args)),
        mesh=mesh, in_specs=in_specs, out_specs=out_specs, check_vma=False,
    )
```

```python
import functools

import jax
import jax.numpy as jnp
from jax import lax
from jax.experimental import pallas as pl
from jax.experimental.pallas import tpu as pltpu
from jax.sharding import PartitionSpec as P

LANES = 128
TINY = 1.1754944e-38


def divisor(n, most):
    return max(d for d in range(1, min(n, most) + 1) if n % d == 0)


def swap(x, axis, bit):
    n = lax.axis_size(axis)
    return lax.ppermute(x, axis, [(i, i ^ bit) for i in range(n)])


def bits_down(n):
    return [1 << b for b in reversed(range(n.bit_length() - 1))]


def gather_all(block, pairs):
    frames, feats = lax.axis_size("frame"), lax.axis_size("feat")
    f, g = lax.axis_index("frame"), lax.axis_index("feat")
    lanes = block.shape[-1]
    held = block[None]
    for bit in bits_down(frames):
        got = swap(held, "frame", bit)
        held = jnp.stack([held, got], axis=1).reshape((-1,) + block.shape)
    share = frames // feats
    width = pairs.shape[1] // share
    piece = lax.dynamic_slice_in_dim(pairs, (f % share) * width, width, 1)
    piece = piece.astype(block.dtype).reshape(-1, lanes)
    wanted = f // share
    for bit in bits_down(feats):
        rows = held.reshape(-1, lanes)
        got = swap(jnp.concatenate([rows, piece], axis=0), "feat", bit)
        held = jnp.concatenate([held, got[: rows.shape[0]].reshape(held.shape)], axis=2)
        piece = jnp.where((wanted & bit) == (g & bit), piece, got[rows.shape[0] :])
    return held, piece


def covariances(
    lag, tile, chunk, f_ref, y_ref, pairs_ref, cols_ref, inst_hbm, lag_hbm,
    x_ref, xt_ref, r_ref, la_ref, lb_ref, out_ref, sems,
):
    frames, _, replicas, blocks = y_ref.shape
    samples = frames * replicas
    row_width, col_width = pairs_ref.shape[1], r_ref.shape[1]
    steps, chunks = row_width // tile, col_width // chunk
    early = (frames - lag) * replicas
    late = lag * replicas
    f = f_ref[0]
    sides = (la_ref, lb_ref)

    walkers = lax.broadcasted_iota(jnp.int32, (replicas, replicas), 1).astype(jnp.float32)
    for t in range(frames):
        slab = y_ref.at[t ^ f]
        labels = slab[3][:, :replicas].astype(jnp.float32)
        match = jnp.where(labels == walkers, 1.0, 0.0).astype(jnp.bfloat16)
        for c in range(3):
            part = lax.dot_general(
                match, slab[c], (((0,), (0,)), ((), ())), preferred_element_type=jnp.float32
            )
            at = (t * 3 + c) * replicas
            x_ref[at : at + replicas, :] = part.astype(jnp.bfloat16)
            xt_ref[c, t] = part.T.astype(jnp.bfloat16)

    def root(x):
        return x * lax.rsqrt(jnp.maximum(x, TINY))

    ids = lax.broadcasted_iota(jnp.int32, (blocks, LANES), 0)
    idsf = ids.astype(jnp.float32)
    half = col_width // LANES

    def pick_cols(j):
        first = cols_ref[j : j + 1, :].astype(jnp.float32)
        second = cols_ref[half + j : half + j + 1, :].astype(jnp.float32)
        return (jnp.where(idsf == first, 1.0, 0.0) - jnp.where(idsf == second, 1.0, 0.0))

    def right(n):
        wide = min(256, chunk)
        for k in range(n * chunk, (n + 1) * chunk, wide):
            pick = jnp.concatenate(
                [pick_cols(k // LANES + i) for i in range(wide // LANES)], axis=1
            ).astype(jnp.bfloat16)
            parts = jnp.dot(x_ref[...], pick, preferred_element_type=jnp.float32)
            parts = parts.reshape(frames, 3, replicas, wide)
            values = root(jnp.sum(parts * parts, axis=1)).reshape(samples, wide)
            mean = jnp.sum(values, axis=0, keepdims=True) * (1.0 / samples)
            r_ref[:, k : k + wide] = (values - mean).astype(jnp.bfloat16)

    def left(step, l_ref, part, parts):
        rows = tile // parts
        picks = []
        for j in range(rows // LANES):
            at = pl.ds(pl.multiple_of(step * tile + part * rows + j * LANES, LANES), LANES)
            first = jnp.where(ids == pairs_ref[0:1, at], 1.0, 0.0)
            second = jnp.where(ids == pairs_ref[1:2, at], 1.0, 0.0)
            picks.append((first - second).T.astype(jnp.bfloat16))
        pick = jnp.concatenate(picks, axis=0)
        total = None
        for c in range(3):
            xt = jnp.concatenate([xt_ref[c, t] for t in range(frames)], axis=1)
            d = jnp.dot(pick, xt, preferred_element_type=jnp.float32)
            total = d * d if total is None else total + d * d
        values = root(total)
        mean = jnp.sum(values, axis=1, keepdims=True) * (1.0 / samples)
        l_ref[part * rows : (part + 1) * rows, :] = (values - mean).astype(jnp.bfloat16)

    def copies(step, slot, n):
        rows = pl.ds(pl.multiple_of(step * tile, tile), tile)
        at = pl.ds(n * chunk, chunk)
        return [
            pltpu.make_async_copy(
                out_ref.at[slot, o, :, at], hbm.at[rows, at], sems.at[slot, o, n]
            )
            for o, hbm in enumerate((inst_hbm, lag_hbm))
        ]

    def products(l_ref, slot, n):
        at = slice(n * chunk, (n + 1) * chunk)
        out_ref[slot, 0, :, at] = jnp.dot(
            l_ref[...], r_ref[:, at], preferred_element_type=jnp.float32
        ) * (1.0 / samples)
        out_ref[slot, 1, :, at] = jnp.dot(
            l_ref[:, :early], r_ref[late:, at], preferred_element_type=jnp.float32
        ) * (1.0 / early)

    def round_of(step, slot, first=False, wait=True, last=False):
        if wait:
            for n in range(chunks):
                for copy in copies(step - 2, slot, n):
                    copy.wait()
        for n in range(chunks):
            products(sides[slot], slot, n)
            if first and n + 1 < chunks:
                right(n + 1)
            if not last:
                left(step + 1, sides[1 - slot], n, chunks)
            for copy in copies(step, slot, n):
                copy.start()

    left(0, la_ref, 0, 1)
    right(0)
    if steps % 2:
        raise ValueError("odd steps")
    round_of(0, 0, first=True, wait=False)
    round_of(1, 1, wait=False, last=steps == 2)
    if steps > 2:
        def body(i, carry):
            round_of(2 * i, 0)
            round_of(2 * i + 1, 1)
            return carry

        lax.fori_loop(1, steps // 2 - 1, body, 0)
        round_of(steps - 2, 0)
        round_of(steps - 1, 1, last=True)
    for step in (steps - 2, steps - 1):
        for n in range(chunks):
            for copy in copies(step, step % 2, n):
                copy.wait()


def per_device(coords, walker_map, pairs):
    frames, feats = lax.axis_size("frame"), lax.axis_size("feat")
    blocks = coords.shape[3]
    row_width = pairs.shape[1]
    col_width = row_width * feats // frames
    labels = jnp.broadcast_to(walker_map[0][:, None], (walker_map.shape[1], blocks))
    block = jnp.concatenate(
        [jnp.swapaxes(coords[0], 0, 1), labels.astype(coords.dtype)[None]], axis=0
    )
    held, cols = gather_all(block, pairs)
    replicas = held.shape[2]
    samples = frames * replicas
    tile, chunk = divisor(row_width // 2, 512), divisor(col_width, 512)
    vmem = pl.BlockSpec(memory_space=pltpu.VMEM)
    hbm = pl.BlockSpec(memory_space=pl.ANY)
    return pl.pallas_call(
        functools.partial(covariances, frames // 3, tile, chunk),
        out_shape=[jax.ShapeDtypeStruct((row_width, col_width), jnp.float32)] * 2,
        in_specs=[pl.BlockSpec(memory_space=pltpu.SMEM), vmem, vmem, vmem],
        out_specs=[hbm, hbm],
        scratch_shapes=[
            pltpu.VMEM((samples * 3, blocks), jnp.bfloat16),
            pltpu.VMEM((3, frames, blocks, replicas), jnp.bfloat16),
            pltpu.VMEM((samples, col_width), jnp.bfloat16),
            pltpu.VMEM((tile, samples), jnp.bfloat16),
            pltpu.VMEM((tile, samples), jnp.bfloat16),
            pltpu.VMEM((2, 2, tile, col_width), jnp.float32),
            pltpu.SemaphoreType.DMA((2, 2, col_width // chunk)),
        ],
        compiler_params=pltpu.CompilerParams(vmem_limit_bytes=52 << 20),
    )(lax.axis_index("frame").astype(jnp.int32).reshape(1), held, pairs, cols)


def solution(mesh):
    in_specs = (P("frame", "feat", None, None), P("frame", "feat"), P(None, "feat"))
    out_specs = (P("feat", "frame"), P("feat", "frame"))
    return jax.shard_map(
        lambda *args: tuple(per_device(*args)),
        mesh=mesh, in_specs=in_specs, out_specs=out_specs, check_vma=False,
    )
```

```python
import functools

import jax
import jax.numpy as jnp
from jax import lax
from jax.experimental import pallas as pl
from jax.experimental.pallas import tpu as pltpu
from jax.sharding import PartitionSpec as P

LANES = 128
TINY = 1.1754944e-38


def divisor(n, most):
    return max(d for d in range(1, min(n, most) + 1) if n % d == 0)


def swap(x, axis, bit):
    n = lax.axis_size(axis)
    return lax.ppermute(x, axis, [(i, i ^ bit) for i in range(n)])


def bits_down(n):
    return [1 << b for b in reversed(range(n.bit_length() - 1))]


def gather_all(block, pairs):
    frames, feats = lax.axis_size("frame"), lax.axis_size("feat")
    f, g = lax.axis_index("frame"), lax.axis_index("feat")
    lanes = block.shape[-1]
    held = block[None]
    for bit in bits_down(frames)[:-1]:
        got = swap(held, "frame", bit)
        held = jnp.stack([held, got], axis=1).reshape((-1,) + block.shape)
    share = frames // feats
    width = pairs.shape[1] // share
    piece = lax.dynamic_slice_in_dim(pairs, (f % share) * width, width, 1)
    piece = piece.reshape(-1, lanes)
    wanted = f // share

    def feat_hop(held, piece, bit):
        rows = held.reshape(-1, lanes)
        got = swap(jnp.concatenate([rows, piece], axis=0), "feat", bit)
        piece = jnp.where((wanted & bit) == (g & bit), piece, got[rows.shape[0] :])
        return got[: rows.shape[0]].reshape(held.shape), piece

    def corner(x):
        both = [
            (i * feats + j, (i ^ 1) * feats + (j ^ 2)) for i in range(frames) for j in range(feats)
        ]
        return lax.ppermute(x, ("frame", "feat"), both)

    for bit in bits_down(feats)[:-2]:
        got, piece = feat_hop(held, piece, bit)
        held = jnp.concatenate([held, got], axis=2)
    far = corner(held)
    near, piece = feat_hop(held, piece, 2)
    side = swap(held, "frame", 1)
    held = jnp.stack(
        [jnp.concatenate([held, near], axis=2), jnp.concatenate([side, far], axis=2)], axis=1
    )
    held = held.reshape((frames,) + held.shape[2:])
    got, piece = feat_hop(held, piece, 1)
    return jnp.concatenate([held, got], axis=2), piece


def covariances(
    lag, count, tile, chunk, f_ref, y_ref, pairs_ref, cols_ref, inst_hbm, lag_hbm,
    x_ref, xt_ref, r_ref, la_ref, lb_ref, out_ref, sems,
):
    frames, _, replicas, blocks = y_ref.shape
    samples = frames * replicas
    row_width, col_width = pairs_ref.shape[1], r_ref.shape[1]
    steps, chunks = row_width // tile, col_width // chunk
    early = (frames - lag) * replicas
    late = lag * replicas
    f = f_ref[0]
    sides = (la_ref, lb_ref)

    walkers = lax.broadcasted_iota(jnp.int32, (replicas, blocks), 0).astype(jnp.float32)
    for t in range(frames):
        slab = y_ref.at[t ^ f]
        labels = slab[3, 0:1, :].astype(jnp.float32)
        for b in range(count, replicas, count):
            labels += pltpu.roll(slab[3, b : b + 1, :].astype(jnp.float32), b, 1)
        match = jnp.where(labels == walkers, 1.0, 0.0)[:, :replicas].astype(jnp.bfloat16)
        for c in range(3):
            part = jnp.dot(match, slab[c], preferred_element_type=jnp.float32)
            at = (t * 3 + c) * replicas
            x_ref[at : at + replicas, :] = part.astype(jnp.bfloat16)
            xt_ref[c, t] = part.T.astype(jnp.bfloat16)

    def root(x):
        return x * lax.rsqrt(jnp.maximum(x, TINY))

    idsf = lax.broadcasted_iota(jnp.int32, (blocks, LANES), 0).astype(jnp.float32)
    half = col_width // LANES

    def pick_cols(j):
        first = cols_ref[j : j + 1, :].astype(jnp.float32)
        second = cols_ref[half + j : half + j + 1, :].astype(jnp.float32)
        return (jnp.where(idsf == first, 1.0, 0.0) - jnp.where(idsf == second, 1.0, 0.0))

    def right(n):
        wide = min(256, chunk)
        for k in range(n * chunk, (n + 1) * chunk, wide):
            pick = jnp.concatenate(
                [pick_cols(k // LANES + i) for i in range(wide // LANES)], axis=1
            ).astype(jnp.bfloat16)
            parts = jnp.dot(x_ref[...], pick, preferred_element_type=jnp.float32)
            parts = parts.reshape(frames, 3, replicas, wide)
            values = root(jnp.sum(parts * parts, axis=1)).reshape(samples, wide)
            mean = jnp.sum(values, axis=0, keepdims=True) * (1.0 / samples)
            r_ref[:, k : k + wide] = (values - mean).astype(jnp.bfloat16)

    def left(step, l_ref, part, parts):
        rows = tile // parts
        picks = []
        for j in range(rows // LANES):
            at = pl.ds(pl.multiple_of(step * tile + part * rows + j * LANES, LANES), LANES)
            both = pairs_ref[:, at].astype(jnp.float32)
            first = jnp.where(idsf == both[0:1], 1.0, 0.0)
            second = jnp.where(idsf == both[1:2], 1.0, 0.0)
            picks.append((first - second).T.astype(jnp.bfloat16))
        pick = jnp.concatenate(picks, axis=0)
        total = None
        for c in range(3):
            xt = jnp.concatenate([xt_ref[c, t] for t in range(frames)], axis=1)
            d = jnp.dot(pick, xt, preferred_element_type=jnp.float32)
            total = d * d if total is None else total + d * d
        values = root(total)
        mean = jnp.sum(values, axis=1, keepdims=True) * (1.0 / samples)
        l_ref[part * rows : (part + 1) * rows, :] = (values - mean).astype(jnp.bfloat16)

    def copies(step, slot, n):
        rows = pl.ds(pl.multiple_of(step * tile, tile), tile)
        at = pl.ds(n * chunk, chunk)
        return [
            pltpu.make_async_copy(
                out_ref.at[slot, o, :, at], hbm.at[rows, at], sems.at[slot, o, n]
            )
            for o, hbm in enumerate((inst_hbm, lag_hbm))
        ]

    def products(l_ref, slot, n):
        at = slice(n * chunk, (n + 1) * chunk)
        out_ref[slot, 0, :, at] = jnp.dot(
            l_ref[...], r_ref[:, at], preferred_element_type=jnp.float32
        ) * (1.0 / samples)
        out_ref[slot, 1, :, at] = jnp.dot(
            l_ref[:, :early], r_ref[late:, at], preferred_element_type=jnp.float32
        ) * (1.0 / early)

    def round_of(step, slot, first=False, wait=True, last=False):
        if wait:
            for n in range(chunks):
                for copy in copies(step - 2, slot, n):
                    copy.wait()
        for n in range(chunks):
            products(sides[slot], slot, n)
            if first and n + 1 < chunks:
                right(n + 1)
            if not last:
                left(step + 1, sides[1 - slot], n, chunks)
            for copy in copies(step, slot, n):
                copy.start()

    left(0, la_ref, 0, 1)
    right(0)
    if steps % 2:
        raise ValueError("odd steps")
    round_of(0, 0, first=True, wait=False)
    round_of(1, 1, wait=False, last=steps == 2)
    if steps > 2:
        def body(i, carry):
            round_of(2 * i, 0)
            round_of(2 * i + 1, 1)
            return carry

        lax.fori_loop(1, steps // 2 - 1, body, 0)
        round_of(steps - 2, 0)
        round_of(steps - 1, 1, last=True)
    for step in (steps - 2, steps - 1):
        for n in range(chunks):
            for copy in copies(step, step % 2, n):
                copy.wait()


def per_device(coords, walker_map, pairs):
    frames, feats = lax.axis_size("frame"), lax.axis_size("feat")
    blocks = coords.shape[3]
    row_width = pairs.shape[1]
    col_width = row_width * feats // frames
    own = jnp.swapaxes(coords[0], 0, 1)
    count = own.shape[1]
    labels = jnp.pad(walker_map.astype(own.dtype), ((0, count - 1), (0, blocks - count)))
    block = jnp.concatenate([own, labels[None]], axis=0)
    pairs = lax.optimization_barrier(pairs.astype(own.dtype))
    held, cols = gather_all(block, pairs)
    replicas = held.shape[2]
    samples = frames * replicas
    tile, chunk = divisor(row_width // 2, 512), divisor(col_width, 512)
    vmem = pl.BlockSpec(memory_space=pltpu.VMEM)
    hbm = pl.BlockSpec(memory_space=pl.ANY)
    return pl.pallas_call(
        functools.partial(covariances, frames // 3, count, tile, chunk),
        out_shape=[jax.ShapeDtypeStruct((row_width, col_width), jnp.float32)] * 2,
        in_specs=[pl.BlockSpec(memory_space=pltpu.SMEM), vmem, vmem, vmem],
        out_specs=[hbm, hbm],
        scratch_shapes=[
            pltpu.VMEM((samples * 3, blocks), jnp.bfloat16),
            pltpu.VMEM((3, frames, blocks, replicas), jnp.bfloat16),
            pltpu.VMEM((samples, col_width), jnp.bfloat16),
            pltpu.VMEM((tile, samples), jnp.bfloat16),
            pltpu.VMEM((tile, samples), jnp.bfloat16),
            pltpu.VMEM((2, 2, tile, col_width), jnp.float32),
            pltpu.SemaphoreType.DMA((2, 2, col_width // chunk)),
        ],
        compiler_params=pltpu.CompilerParams(vmem_limit_bytes=52 << 20),
    )(lax.axis_index("frame").astype(jnp.int32).reshape(1), held, pairs, cols)


def solution(mesh):
    in_specs = (P("frame", "feat", None, None), P("frame", "feat"), P(None, "feat"))
    out_specs = (P("feat", "frame"), P("feat", "frame"))
    return jax.shard_map(
        lambda *args: tuple(per_device(*args)),
        mesh=mesh, in_specs=in_specs, out_specs=out_specs, check_vma=False,
    )
```

```python
import functools

import jax
import jax.numpy as jnp
from jax import lax
from jax.experimental import pallas as pl
from jax.experimental.pallas import tpu as pltpu
from jax.sharding import PartitionSpec as P

LANES = 128
TINY = 1.1754944e-38


def divisor(n, most):
    return max(d for d in range(1, min(n, most) + 1) if n % d == 0)


def swap(x, axis, bit):
    n = lax.axis_size(axis)
    return lax.ppermute(x, axis, [(i, i ^ bit) for i in range(n)])


def bits_down(n):
    return [1 << b for b in reversed(range(n.bit_length() - 1))]


def gather_all(block, pairs):
    frames, feats = lax.axis_size("frame"), lax.axis_size("feat")
    f, g = lax.axis_index("frame"), lax.axis_index("feat")
    lanes = block.shape[-1]
    held = block[None]
    for bit in bits_down(frames)[:-1]:
        got = swap(held, "frame", bit)
        held = jnp.stack([held, got], axis=1).reshape((-1,) + block.shape)
    share = frames // feats
    width = pairs.shape[1] // share
    piece = lax.dynamic_slice_in_dim(pairs, (f % share) * width, width, 1)
    piece = piece.reshape(-1, lanes)
    wanted = f // share

    def feat_hop(held, piece, bit):
        rows = held.reshape(-1, lanes)
        got = swap(jnp.concatenate([rows, piece], axis=0), "feat", bit)
        piece = jnp.where((wanted & bit) == (g & bit), piece, got[rows.shape[0] :])
        return got[: rows.shape[0]].reshape(held.shape), piece

    def corner(x):
        both = [
            (i * feats + j, (i ^ 1) * feats + (j ^ 2)) for i in range(frames) for j in range(feats)
        ]
        return lax.ppermute(x, ("frame", "feat"), both)

    for bit in bits_down(feats)[:-2]:
        got, piece = feat_hop(held, piece, bit)
        held = jnp.concatenate([held, got], axis=2)
    far = corner(held)
    near, piece = feat_hop(held, piece, 2)
    side = swap(held, "frame", 1)
    held = jnp.stack(
        [jnp.concatenate([held, near], axis=2), jnp.concatenate([side, far], axis=2)], axis=1
    )
    held = held.reshape((frames,) + held.shape[2:])
    got, piece = feat_hop(held, piece, 1)
    return jnp.concatenate([held, got], axis=2), piece


def covariances(
    lag, count, tile, chunk, f_ref, y_ref, pairs_ref, cols_ref, inst_hbm, lag_hbm,
    x_ref, xt_ref, r_ref, la_ref, lb_ref, out_ref, sems,
):
    frames, _, replicas, blocks = y_ref.shape
    samples = frames * replicas
    row_width, col_width = pairs_ref.shape[1], r_ref.shape[1]
    steps, chunks = row_width // tile, col_width // chunk
    early = (frames - lag) * replicas
    late = lag * replicas
    f = f_ref[0]
    sides = (la_ref, lb_ref)
    slots = out_ref.shape[0]

    walkers = lax.broadcasted_iota(jnp.int32, (replicas, blocks), 0).astype(jnp.float32)
    for t in range(frames):
        slab = y_ref.at[t ^ f]
        labels = slab[3, 0:1, :].astype(jnp.float32)
        for b in range(count, replicas, count):
            labels += pltpu.roll(slab[3, b : b + 1, :].astype(jnp.float32), b, 1)
        match = jnp.where(labels == walkers, 1.0, 0.0)[:, :replicas].astype(jnp.bfloat16)
        for c in range(3):
            part = jnp.dot(match, slab[c], preferred_element_type=jnp.float32)
            at = (t * 3 + c) * replicas
            x_ref[at : at + replicas, :] = part.astype(jnp.bfloat16)
            xt_ref[c, t] = part.T.astype(jnp.bfloat16)

    def root(x):
        return x * lax.rsqrt(jnp.maximum(x, TINY))

    idsf = lax.broadcasted_iota(jnp.int32, (blocks, LANES), 0).astype(jnp.float32)
    half = col_width // LANES

    def pick_cols(j):
        first = cols_ref[j : j + 1, :].astype(jnp.float32)
        second = cols_ref[half + j : half + j + 1, :].astype(jnp.float32)
        return (jnp.where(idsf == first, 1.0, 0.0) - jnp.where(idsf == second, 1.0, 0.0))

    def right(n):
        wide = min(256, chunk)
        for k in range(n * chunk, (n + 1) * chunk, wide):
            pick = jnp.concatenate(
                [pick_cols(k // LANES + i) for i in range(wide // LANES)], axis=1
            ).astype(jnp.bfloat16)
            parts = jnp.dot(x_ref[...], pick, preferred_element_type=jnp.float32)
            parts = parts.reshape(frames, 3, replicas, wide)
            values = root(jnp.sum(parts * parts, axis=1)).reshape(samples, wide)
            mean = jnp.sum(values, axis=0, keepdims=True) * (1.0 / samples)
            r_ref[:, k : k + wide] = (values - mean).astype(jnp.bfloat16)

    def left(step, l_ref):
        picks = []
        for j in range(tile // LANES):
            at = pl.ds(step * tile + j * LANES, LANES)
            both = pairs_ref[:, at].astype(jnp.float32)
            first = jnp.where(idsf == both[0:1], 1.0, 0.0)
            second = jnp.where(idsf == both[1:2], 1.0, 0.0)
            picks.append((first - second).T.astype(jnp.bfloat16))
        pick = jnp.concatenate(picks, axis=0)
        total = None
        for c in range(3):
            xt = jnp.concatenate([xt_ref[c, t] for t in range(frames)], axis=1)
            d = jnp.dot(pick, xt, preferred_element_type=jnp.float32)
            total = d * d if total is None else total + d * d
        values = root(total)
        mean = jnp.sum(values, axis=1, keepdims=True) * (1.0 / samples)
        l_ref[...] = (values - mean).astype(jnp.bfloat16)

    def copies(step, slot, n):
        rows = pl.ds(step * tile, tile)
        at = pl.ds(n * chunk, chunk)
        return [
            pltpu.make_async_copy(
                out_ref.at[slot, o, :, at], hbm.at[rows, at], sems.at[slot, o, n]
            )
            for o, hbm in enumerate((inst_hbm, lag_hbm))
        ]

    def products(l_ref, slot, n):
        at = slice(n * chunk, (n + 1) * chunk)
        out_ref[slot, 0, :, at] = jnp.dot(
            l_ref[...], r_ref[:, at], preferred_element_type=jnp.float32
        ) * (1.0 / samples)
        out_ref[slot, 1, :, at] = jnp.dot(
            l_ref[:, :early], r_ref[late:, at], preferred_element_type=jnp.float32
        ) * (1.0 / early)

    def send(step, slot, n):
        for copy in copies(step, slot, n):
            copy.start()

    def collect(step):
        for n in range(chunks):
            for copy in copies(step, step % slots, n):
                copy.wait()

    left(0, la_ref)
    right(0)
    left(1, lb_ref)
    for n in range(chunks):
        if n + 1 < chunks:
            right(n + 1)
        products(la_ref, 0, n)
        send(0, 0, n)
        if n + 1 == chunks and steps > 2:
            left(2, la_ref)
        products(lb_ref, 1, n)
        send(1, 1, n)
    for step in range(2, steps):
        if step >= slots and step % 2 == 0:
            for old in range(step - slots, min(step - slots + 2, steps)):
                collect(old)
        for n in range(chunks):
            products(sides[step % 2], step % slots, n)
            if step + 1 < steps and n == 0:
                left(step + 1, sides[(step + 1) % 2])
            send(step, step % slots, n)
    for step in range(steps - slots, steps):
        collect(step)


def per_device(coords, walker_map, pairs):
    frames, feats = lax.axis_size("frame"), lax.axis_size("feat")
    blocks = coords.shape[3]
    row_width = pairs.shape[1]
    col_width = row_width * feats // frames
    own = jnp.swapaxes(coords[0], 0, 1)
    count = own.shape[1]
    labels = jnp.pad(walker_map.astype(own.dtype), ((0, count - 1), (0, blocks - count)))
    block = jnp.concatenate([own, labels[None]], axis=0)
    pairs = lax.optimization_barrier(pairs.astype(own.dtype))
    held, cols = gather_all(block, pairs)
    replicas = held.shape[2]
    samples = frames * replicas
    tile, chunk = divisor(row_width // 2, 512), divisor(col_width, 512)
    slots = min(row_width // tile, 4)
    vmem = pl.BlockSpec(memory_space=pltpu.VMEM)
    hbm = pl.BlockSpec(memory_space=pl.ANY)
    return pl.pallas_call(
        functools.partial(covariances, frames // 3, count, tile, chunk),
        out_shape=[jax.ShapeDtypeStruct((row_width, col_width), jnp.float32)] * 2,
        in_specs=[pl.BlockSpec(memory_space=pltpu.SMEM), vmem, vmem, vmem],
        out_specs=[hbm, hbm],
        scratch_shapes=[
            pltpu.VMEM((samples * 3, blocks), jnp.bfloat16),
            pltpu.VMEM((3, frames, blocks, replicas), jnp.bfloat16),
            pltpu.VMEM((samples, col_width), jnp.bfloat16),
            pltpu.VMEM((tile, samples), jnp.bfloat16),
            pltpu.VMEM((tile, samples), jnp.bfloat16),
            pltpu.VMEM((slots, 2, tile, col_width), jnp.float32),
            pltpu.SemaphoreType.DMA((slots, 2, col_width // chunk)),
        ],
        compiler_params=pltpu.CompilerParams(vmem_limit_bytes=52 << 20),
    )(lax.axis_index("frame").astype(jnp.int32).reshape(1), held, pairs, cols)


def solution(mesh):
    in_specs = (P("frame", "feat", None, None), P("frame", "feat"), P(None, "feat"))
    out_specs = (P("feat", "frame"), P("feat", "frame"))
    return jax.shard_map(
        lambda *args: tuple(per_device(*args)),
        mesh=mesh, in_specs=in_specs, out_specs=out_specs, check_vma=False,
    )
```
